32 devices in a mesh: row: 4 (over z), col: 4 (over y, x), layer: 2 (over core).
Axes of the slice: x: 2, y: 2, z: 4, core: 2. Of those that a mesh axis runs over, the one named last changes fastest.
Arguments:
- ratings: bfloat16 [8192, 4096], P('row', ('col', 'layer')), may hold values from -6 to 6
- tile_mask: int32 [64, 32], P('row', ('col', 'layer')), may hold values 0 or 1
- tile_counts: int32 [64, 32], P('row', ('col', 'layer')), may hold values from 1 to 16384
- user_factor: float32 [256, 8192], P(('col', 'layer'), 'row'), may hold values from -1.5 to 1.5
- item_factor: float32 [256, 4096], P('row', ('col', 'layer')), may hold values from -1.5 to 1.5
Outputs:
- new_user: float32 [256, 8192], P(('col', 'layer'), 'row')
- new_item: float32 [256, 4096], P('row', ('col', 'layer'))
- loss_value: float32 [], replicated
- grad_norm: float32 [], replicated
The draws below stay inside these ranges and needn't reach their ends.
All inputs are finite; a program needn't handle non-finite values. No bound on the sum of `tile_mask` on one device may be relied on, other than what follows from the above.
Results may differ from the reference program's by a relative error of at most 0.0049.
Values may be sent and summed in bfloat16 or wider, within the bound.
A program may use at most 64 MiB of HBM per device.

```python
import jax
import jax.numpy as jnp
from jax import lax

K = 256
TILE = 128
BR = 2048
NR = 8192
NC = 4096


def place_ends(result, stream_key, least, high):
    extent = result.shape
    spot = [jax.random.randint(jax.random.fold_in(stream_key, axis), (), 0, extent[axis]) for axis in range(len(extent))]
    result = result.at[tuple(spot)].set(least)
    longest = extent.index(max(extent))
    spot[longest] = (spot[longest] + 1) % extent[longest]
    return result.at[tuple(spot)].set(high)


def level_of(key, dims, cuts, least, high):
    factor_of, own = 1.0, jax.random.fold_in(key, 6)
    for axis_at, shards_of in cuts:
        heights = jnp.exp(jax.random.uniform(jax.random.fold_in(own, axis_at), (shards_of,), jnp.float32, least / len(cuts), high / len(cuts)))
        factor_of = factor_of * jnp.repeat(heights, dims[axis_at] // shards_of).reshape([-1 if axis == axis_at else 1 for axis in range(len(dims))])
    return factor_of


def gaussian(key, shape, spread, limit, split=(), dtype=jnp.bfloat16):
    drawn = jax.random.normal(key, shape, jnp.float32) * spread
    if len(split) > 0:
        drawn = level_of(key, shape, split, -0.22, 0.18) * drawn
    return jnp.clip(drawn, min=-limit, max=limit).astype(dtype)


def setup_inputs(seed: int = 0) -> dict:
    splits = jax.random.split(jax.random.key(seed), 6)
    return {
        "ratings": gaussian(splits[0], (NR, NC), 1.0, 6.0, ((0, 4), (1, 8))),
        "tile_mask": place_ends((jax.random.randint(splits[1], (NR // TILE, NC // TILE), 0, 4) < 3).astype(jnp.int32), jax.random.fold_in(splits[1], 1), 0, 1),
        "tile_counts": place_ends(jax.random.randint(splits[2], (NR // TILE, NC // TILE), 1, TILE * TILE + 1), jax.random.fold_in(splits[2], 1), 1, TILE * TILE).astype(jnp.int32),
        "user_factor": gaussian(splits[3], (K, NR), 0.25, 1.5, ((0, 8), (1, 4)), jnp.float32),
        "item_factor": gaussian(splits[4], (K, NC), 0.25, 1.5, ((0, 4), (1, 8)), jnp.float32),
    }


epsilon = 1e-12
trust_ratio = 0.2

def tile_weights(mask_rows, count_rows):
    position = lax.broadcasted_iota(jnp.int32, (TILE, TILE), 0) * TILE + lax.broadcasted_iota(jnp.int32, (TILE, TILE), 1)
    observed = (mask_rows[:, None, :, None] == 1) & (position[None, :, None, :] < count_rows[:, None, :, None])
    return observed.astype(jnp.float32).reshape(mask_rows.shape[0] * TILE, mask_rows.shape[1] * TILE)

def reference(ratings, tile_mask, tile_counts, user_factor, item_factor):
    user_low = user_factor.astype(jnp.bfloat16)
    item_low = item_factor.astype(jnp.bfloat16)
    observed_total = jnp.maximum(jnp.sum(tile_mask * tile_counts).astype(jnp.float32), jnp.float32(1.0))
    blocks = NR // BR

    def advance(running, block_index):
        error_sum, raw_item = running
        offset = (block_index * BR).astype(jnp.int32)
        tile_offset = (block_index * (BR // TILE)).astype(jnp.int32)
        rating_rows = lax.dynamic_slice_in_dim(ratings, offset, BR, 0)
        mask_rows = lax.dynamic_slice_in_dim(tile_mask, tile_offset, BR // TILE, 0)
        count_rows = lax.dynamic_slice_in_dim(tile_counts, tile_offset, BR // TILE, 0)
        user_rows = lax.dynamic_slice_in_dim(user_low, offset, BR, 1)
        predicted = lax.dot_general(user_rows, item_low, (((0,), (0,)), ((), ())), preferred_element_type=jnp.float32)
        residual = tile_weights(mask_rows, count_rows) * (predicted - rating_rows.astype(jnp.float32))
        scaled = residual.astype(jnp.bfloat16)
        raw_user = lax.dot_general(item_low, scaled, (((1,), (1,)), ((), ())), preferred_element_type=jnp.float32)
        raw_item = raw_item + jnp.dot(user_rows, scaled, preferred_element_type=jnp.float32)
        return ((error_sum + jnp.sum(residual * residual), raw_item), raw_user)
    start_state = (jnp.float32(0.0), jnp.zeros((K, NC), jnp.float32))
    (error_sum, raw_item), user_blocks = lax.scan(advance, start_state, jnp.arange(blocks).astype(jnp.int32))
    raw_user = jnp.transpose(user_blocks, (1, 0, 2)).reshape(K, NR)
    loss_value = error_sum / observed_total
    grad_norm = 2.0 / observed_total * jnp.sqrt(jnp.sum(raw_user * raw_user) + jnp.sum(raw_item * raw_item) + epsilon)
    factor_norm = jnp.sqrt(jnp.sum(user_factor * user_factor) + jnp.sum(item_factor * item_factor) + epsilon)
    rate = trust_ratio * factor_norm / grad_norm
    step_size = rate * (2.0 / observed_total)
    new_user = user_factor - step_size * raw_user
    new_item = item_factor - step_size * raw_item
    return (new_user, new_item, loss_value, grad_norm)
```

```python
import math

import jax
import jax.numpy as jnp
from jax import lax
from jax.experimental import pallas as pl
from jax.experimental.pallas import tpu as pltpu
from jax.sharding import PartitionSpec as P

TILE = 128
epsilon = 1e-12
trust_ratio = 0.2
MESH = pl.DeviceIdType.MESH
CHUNKS = 4


def fold(value):
    flat = value.reshape(-1, value.shape[-1])
    rows = jnp.sum(flat.reshape(flat.shape[0] // 8, 8, flat.shape[1]), axis=0)
    total = rows[:, :TILE]
    for start in range(TILE, rows.shape[1], TILE):
        total = total + rows[:, start : start + TILE]
    return total


def make_step(nrow, ncol, nlay, rank, rows, cols):
    side = math.isqrt(ncol)
    ny = nx = side
    if side * side != ncol:
        ny, nx = 1, ncol
    ndev = nrow * ncol * nlay
    nplane = ncol * nlay
    urows, irows = rank // nplane, rank // nrow
    udt = jnp.bfloat16 if urows % 16 == 0 else jnp.float32
    idt = jnp.bfloat16 if irows % 16 == 0 else jnp.float32
    f32, bf16 = jnp.float32, jnp.bfloat16
    nch = CHUNKS
    width = rows // nch
    half = width // 2

    dxs, dys = range(1, nx), range(1, ny)
    dls, dzs = range(1, nlay), range(1, nrow)
    n_own = len(dxs) + len(dys) + len(dls)
    n_x, n_y = len(dxs), len(dys)
    per_chunk = (
        n_own
        + 2 * n_x * n_y
        + len(dls) * (n_x + n_y + 2 * n_x * n_y)
        + len(dls)
        + 2 * (n_x + n_y)
    )
    n_sems = nch * per_chunk + 2 * len(dzs)

    def kernel(
        mask, counts, ratings, user, item, raw_user, raw_item, stats,
        rat, uf, itf, U, I, pred, scaled, acc, PU, send0, recv0, S,
        send_a, recv_a, send_b, recv_b, SA, SB,
        send_a2, recv_a2, send_b2, recv_b2, out_u, out_i,
        send_i, recv_i, mine, G, rat_sem, in_sem, out_sem, ssem, rsem, gsend, grecv,
    ):
        z, c, l = lax.axis_index("row"), lax.axis_index("col"), lax.axis_index("layer")
        y, x = c // nx, c % nx

        def at(z_, y_, x_, l_):
            return (z_, y_ * nx + x_, l_)

        def xp(dx):
            return at(z, y, (x + dx) % nx, l)

        def yp(dy):
            return at(z, (y + dy) % ny, x, l)

        def lp(dl):
            return at(z, y, x, (l + dl) % nlay)

        def zp(dz):
            return at((z + dz) % nrow, y, x, l)

        def rank_of(y_, x_, l_):
            return (y_ * nx + x_) * nlay + l_

        load_u = pltpu.make_async_copy(user, uf, in_sem.at[0])
        load_i = pltpu.make_async_copy(item, itf, in_sem.at[1])
        load_u.start()
        load_i.start()
        loads = []
        for j in range(nch):
            part = pl.ds(j * width, width)
            load = pltpu.make_async_copy(ratings.at[part], rat.at[part], rat_sem.at[j])
            load.start()
            loads.append(load)

        barrier = pltpu.get_barrier_semaphore()
        peers = (
            [lp(d) for d in dls] + [xp(d) for d in dxs] + [yp(d) for d in dys] + [zp(d) for d in dzs]
        )
        for peer in peers:
            pl.semaphore_signal(barrier, inc=1, device_id=peer, device_id_type=MESH)

        me = rank_of(y, x, l)
        load_i.wait()
        I[z] = itf[...].astype(bf16).astype(idt)
        load_u.wait()
        U[me] = uf[...].astype(bf16).astype(udt)
        pl.semaphore_wait(barrier, len(peers))

        used = [0]
        pending = []

        def send(src, dst, peer):
            n = used[0]
            used[0] += 1
            copy = pltpu.make_async_remote_copy(
                src_ref=src, dst_ref=dst, send_sem=ssem.at[n], recv_sem=rsem.at[n],
                device_id=peer, device_id_type=MESH,
            )
            copy.start()
            pending.append(copy)
            return copy

        gathers_i = [send(I.at[z], I.at[z], zp(d)) for d in dzs]

        got_x, got_y, got_a, got_b, got_l = {}, {}, {}, {}, {}

        def block(j, y_, x_, l_, lo, size):
            return U.at[rank_of(y_, x_, l_), :, pl.ds(j * width + lo, size)]

        def own(j):
            b = block(j, y, x, l, 0, width)
            got_x[j] = [send(b, b, xp(d)) for d in dxs]
            got_y[j] = [send(b, b, yp(d)) for d in dys]
            got_l[j] = [send(b, b, lp(d)) for d in dls]

        def relay(j):
            got_a[j], got_b[j] = [], []
            for dx, copy in zip(dxs, got_x[j]):
                copy.wait_recv()
                sx = (x + nx - dx) % nx
                b = block(j, y, sx, l, 0, half)
                got_a[j] += [send(b, b, yp(d)) for d in dys]
            for dy, copy in zip(dys, got_y[j]):
                copy.wait_recv()
                sy = (y + ny - dy) % ny
                b = block(j, sy, x, l, half, half)
                got_b[j] += [send(b, b, xp(d)) for d in dxs]
            for dx in dxs:
                b = block(j, y, (x + nx - dx) % nx, l, 0, width)
                got_l[j] += [send(b, b, lp(d)) for d in dls]
            for dy in dys:
                b = block(j, (y + ny - dy) % ny, x, l, 0, width)
                got_l[j] += [send(b, b, lp(d)) for d in dls]

        def corner(j):
            n = 0
            for dx in dxs:
                for dy in dys:
                    got_a[j][n].wait_recv()
                    n += 1
                    b = block(j, (y + ny - dy) % ny, (x + nx - dx) % nx, l, 0, half)
                    got_l[j] += [send(b, b, lp(d)) for d in dls]
            n = 0
            for dy in dys:
                for dx in dxs:
                    got_b[j][n].wait_recv()
                    n += 1
                    b = block(j, (y + ny - dy) % ny, (x + nx - dx) % nx, l, half, half)
                    got_l[j] += [send(b, b, lp(d)) for d in dls]

        position = lax.broadcasted_iota(jnp.int32, (TILE, TILE), 0) * TILE + lax.broadcasted_iota(
            jnp.int32, (TILE, TILE), 1
        )
        got_0 = {}

        def compute(j, error):
            for copy in got_l[j]:
                copy.wait_recv()
            if j == 0:
                for copy in gathers_i:
                    copy.wait_recv()
            loads[j].wait()
            items = I[...].reshape(rank, cols).astype(bf16)
            users = U[:, :, j * width : (j + 1) * width].reshape(rank, width).astype(bf16)
            pred[...] = lax.dot_general(
                users, items, (((0,), (0,)), ((), ())), preferred_element_type=f32
            )

            def tiles(t, total):
                local = pl.ds(pl.multiple_of(t * TILE, TILE), TILE)
                whole = pl.ds(pl.multiple_of(j * width + t * TILE, TILE), TILE)
                row = j * (width // TILE) + t
                for k in range(cols // TILE):
                    lane = slice(k * TILE, (k + 1) * TILE)
                    limit = jnp.where(mask[row, k] == 1, counts[row, k], 0)
                    diff = pred[local, lane] - rat[whole, lane].astype(f32)
                    diff = jnp.where(position < limit, diff, 0.0)
                    scaled[local, lane] = diff.astype(bf16)
                    total = total + fold(diff * diff)
                return total

            error = lax.fori_loop(0, width // TILE, tiles, error)
            sc = scaled[...]
            PU[j] = lax.dot_general(
                items, sc, (((1,), (1,)), ((), ())), preferred_element_type=f32
            ).reshape(ncol, nlay, urows, width)
            got_0[j] = []
            for dl in dls:
                send0[j, dl - 1] = PU[j, :, (l + dl) % nlay].astype(udt)
                got_0[j].append(send(send0.at[j, dl - 1], recv0.at[j, dl - 1], lp(dl)))
            grad = jnp.dot(users, sc, preferred_element_type=f32).reshape(nrow, irows, cols)
            if j == 0:
                acc[...] = grad
            else:
                acc[...] += grad
            return error

        got_1a, got_1b, got_2a, got_2b = {}, {}, {}, {}

        def rs1(j):
            total = PU[j, :, l]
            for dl, copy in zip(dls, got_0[j]):
                copy.wait_recv()
                total = total + recv0[j, dl - 1].astype(f32)
            S[j] = total.reshape(ny, nx, urows, width)
            got_1a[j], got_1b[j] = [], []
            for dx in dxs:
                send_a[j, dx - 1] = S[j, :, (x + dx) % nx, :, :half].astype(udt)
                got_1a[j].append(send(send_a.at[j, dx - 1], recv_a.at[j, dx - 1], xp(dx)))
            for dy in dys:
                send_b[j, dy - 1] = S[j, (y + dy) % ny, :, :, half:].astype(udt)
                got_1b[j].append(send(send_b.at[j, dy - 1], recv_b.at[j, dy - 1], yp(dy)))

        def rs2(j):
            total = S[j, :, x, :, :half]
            for dx, copy in zip(dxs, got_1a[j]):
                copy.wait_recv()
                total = total + recv_a[j, dx - 1].astype(f32)
            SA[j] = total
            got_2a[j], got_2b[j] = [], []
            for dy in dys:
                send_a2[j, dy - 1] = SA[j, (y + dy) % ny].astype(udt)
                got_2a[j].append(send(send_a2.at[j, dy - 1], recv_a2.at[j, dy - 1], yp(dy)))
            total = S[j, y, :, :, half:]
            for dy, copy in zip(dys, got_1b[j]):
                copy.wait_recv()
                total = total + recv_b[j, dy - 1].astype(f32)
            SB[j] = total
            for dx in dxs:
                send_b2[j, dx - 1] = SB[j, (x + dx) % nx].astype(udt)
                got_2b[j].append(send(send_b2.at[j, dx - 1], recv_b2.at[j, dx - 1], xp(dx)))

        stores = []

        def rs3(j, grads):
            total = SA[j, y]
            for dy, copy in zip(dys, got_2a[j]):
                copy.wait_recv()
                total = total + recv_a2[j, dy - 1].astype(f32)
            out_u[:, j * width : j * width + half] = total
            grads = grads + fold(total * total)
            total = SB[j, x]
            for dx, copy in zip(dxs, got_2b[j]):
                copy.wait_recv()
                total = total + recv_b2[j, dx - 1].astype(f32)
            out_u[:, j * width + half : (j + 1) * width] = total
            grads = grads + fold(total * total)
            return grads

        error = jnp.zeros((8, TILE), f32)
        grads = jnp.zeros((8, TILE), f32)
        own(0)
        if nch > 1:
            own(1)
        relay(0)
        factor = fold(uf[...] * uf[...]) + fold(itf[...] * itf[...])
        got_z = []
        for j in range(nch + 3):
            if j + 2 < nch:
                own(j + 2)
            if j + 1 < nch:
                relay(j + 1)
            if j < nch:
                corner(j)
                error = compute(j, error)
            if j == nch - 1:
                for dz in dzs:
                    send_i[dz - 1] = acc[(z + dz) % nrow].astype(idt)
                    got_z.append(send(send_i.at[dz - 1], recv_i.at[dz - 1], zp(dz)))
            if 0 <= j - 1 < nch:
                rs1(j - 1)
            if 0 <= j - 2 < nch:
                rs2(j - 2)
            if 0 <= j - 3 < nch:
                grads = rs3(j - 3, grads)

        total = acc[z]
        for dz, copy in zip(dzs, got_z):
            copy.wait_recv()
            total = total + recv_i[dz - 1].astype(f32)
        out_i[...] = total
        grads = grads + fold(total * total)

        store_u = pltpu.make_async_copy(out_u, raw_user, out_sem.at[0])
        store_i = pltpu.make_async_copy(out_i, raw_item, out_sem.at[1])
        store_u.start()
        store_i.start()

        def count_of(t, total):
            for k in range(cols // TILE):
                total = total + jnp.where(mask[t, k] == 1, counts[t, k], 0)
            return total

        count = lax.fori_loop(0, rows // TILE, count_of, jnp.int32(0)).astype(f32)
        sub = lax.broadcasted_iota(jnp.int32, (8, TILE), 0)
        lane = lax.broadcasted_iota(jnp.int32, (8, TILE), 1)

        def spread(value):
            return jnp.broadcast_to(jnp.sum(value, axis=0, keepdims=True), (8, TILE))

        tile = jnp.where((sub == 3) & (lane == 0), count, 0.0)
        tile = jnp.where(sub == 0, spread(error), tile)
        tile = jnp.where(sub == 1, spread(factor), tile)
        tile = jnp.where(sub == 2, spread(grads), tile)
        mine[...] = tile
        flat = (z * ncol + c) * nlay + l
        G[flat] = tile

        def share(delta):
            to = (flat + delta) % ndev
            return pltpu.make_async_remote_copy(
                src_ref=mine, dst_ref=G.at[flat], send_sem=gsend, recv_sem=grecv,
                device_id=(to // nplane, (to // nlay) % ncol, to % nlay), device_id_type=MESH,
            )

        @pl.loop(1, ndev)
        def _(delta):
            share(delta).start()

        every = pl.ds(0, ndev - 1)
        pltpu.make_async_copy(G.at[every], G.at[every], grecv).wait()
        total = jnp.sum(G[...], axis=0)

        def pick(n):
            return jnp.sum(total[n : n + 1], axis=1, keepdims=True)

        error_sum, factor_sum, grad_sum = pick(0), pick(1), pick(2)
        observed = jnp.maximum(pick(3), 1.0)
        loss = error_sum / observed
        grad_norm = 2.0 / observed * jnp.sqrt(grad_sum + epsilon)
        rate = trust_ratio * jnp.sqrt(factor_sum + epsilon) / grad_norm
        step = rate * (2.0 / observed)
        result = jnp.where(sub == 0, loss, jnp.where(sub == 1, grad_norm, step))
        stats[...] = result
        for copy in pending:
            copy.wait_send()
        pltpu.make_async_copy(G.at[every], G.at[every], gsend).wait()
        store_u.wait()
        store_i.wait()

    vm = pltpu.VMEM
    dma = pltpu.SemaphoreType.DMA
    mx, my, ml, mz = max(nx - 1, 1), max(ny - 1, 1), max(nlay - 1, 1), max(nrow - 1, 1)
    smem = pl.BlockSpec(memory_space=pltpu.SMEM)
    hbm = pl.BlockSpec(memory_space=pl.ANY)
    return pl.pallas_call(
        kernel,
        out_shape=(
            jax.ShapeDtypeStruct((urows, rows), f32),
            jax.ShapeDtypeStruct((irows, cols), f32),
            jax.ShapeDtypeStruct((8, TILE), f32),
        ),
        in_specs=[smem, smem, hbm, hbm, hbm],
        out_specs=(hbm, hbm, pl.BlockSpec(memory_space=pltpu.VMEM)),
        scratch_shapes=[
            vm((rows, cols), bf16),
            vm((urows, rows), f32),
            vm((irows, cols), f32),
            vm((nplane, urows, rows), udt),
            vm((nrow, irows, cols), idt),
            vm((width, cols), f32),
            vm((width, cols), bf16),
            vm((nrow, irows, cols), f32),
            vm((nch, ncol, nlay, urows, width), f32),
            vm((nch, ml, ncol, urows, width), udt),
            vm((nch, ml, ncol, urows, width), udt),
            vm((nch, ny, nx, urows, width), f32),
            vm((nch, mx, ny, urows, half), udt),
            vm((nch, mx, ny, urows, half), udt),
            vm((nch, my, nx, urows, half), udt),
            vm((nch, my, nx, urows, half), udt),
            vm((nch, ny, urows, half), f32),
            vm((nch, nx, urows, half), f32),
            vm((nch, my, urows, half), udt),
            vm((nch, my, urows, half), udt),
            vm((nch, mx, urows, half), udt),
            vm((nch, mx, urows, half), udt),
            vm((urows, rows), f32),
            vm((irows, cols), f32),
            vm((mz, irows, cols), idt),
            vm((mz, irows, cols), idt),
            vm((8, TILE), f32),
            vm((ndev, 8, TILE), f32),
            dma((nch,)),
            dma((2,)),
            dma((2,)),
            dma((n_sems,)),
            dma((n_sems,)),
            dma(()),
            dma(()),
        ],
        compiler_params=pltpu.CompilerParams(collective_id=0, has_side_effects=True),
        name="completion_step",
    )


def solution(mesh):
    nrow, ncol, nlay = mesh.shape["row"], mesh.shape["col"], mesh.shape["layer"]

    def body(ratings, tile_mask, tile_counts, user_factor, item_factor):
        rows, cols = ratings.shape
        rank = user_factor.shape[0] * ncol * nlay
        step = make_step(nrow, ncol, nlay, rank, rows, cols)
        raw_user, raw_item, stats = step(tile_mask, tile_counts, ratings, user_factor, item_factor)
        step_size = stats[2, 0]
        new_user = user_factor - step_size * raw_user
        new_item = item_factor - step_size * raw_item
        return (new_user, new_item, stats[0, 0], stats[1, 0])

    return jax.shard_map(
        body,
        mesh=mesh,
        in_specs=(
            P("row", ("col", "layer")),
            P("row", ("col", "layer")),
            P("row", ("col", "layer")),
            P(("col", "layer"), "row"),
            P("row", ("col", "layer")),
        ),
        out_specs=(P(("col", "layer"), "row"), P("row", ("col", "layer")), P(), P()),
        check_vma=False,
    )
```

```python
import math

import jax
import jax.numpy as jnp
from jax import lax
from jax.experimental import pallas as pl
from jax.experimental.pallas import tpu as pltpu
from jax.sharding import PartitionSpec as P

TILE = 128
epsilon = 1e-12
trust_ratio = 0.2
MESH = pl.DeviceIdType.MESH
CHUNKS = 2


def fold(value):
    flat = value.reshape(-1, value.shape[-1])
    rows = jnp.sum(flat.reshape(flat.shape[0] // 8, 8, flat.shape[1]), axis=0)
    total = rows[:, :TILE]
    for start in range(TILE, rows.shape[1], TILE):
        total = total + rows[:, start : start + TILE]
    return total


def make_step(nrow, ncol, nlay, rank, rows, cols):
    side = math.isqrt(ncol)
    ny = nx = side
    if side * side != ncol:
        ny, nx = 1, ncol
    ndev = nrow * ncol * nlay
    nplane = ncol * nlay
    urows, irows = rank // nplane, rank // nrow
    udt = jnp.bfloat16 if urows % 16 == 0 else jnp.float32
    idt = jnp.bfloat16 if irows % 16 == 0 else jnp.float32
    f32, bf16 = jnp.float32, jnp.bfloat16
    nch = CHUNKS
    width = rows // nch
    half = width // 2

    dxs, dys = range(1, nx), range(1, ny)
    dls, dzs = range(1, nlay), range(1, nrow)
    n_own = len(dxs) + len(dys) + len(dls)
    n_x, n_y = len(dxs), len(dys)
    per_chunk = (
        n_own
        + 2 * n_x * n_y
        + len(dls) * (n_x + n_y + 2 * n_x * n_y)
        + len(dls)
        + 2 * (n_x + n_y)
    )
    n_sems = nch * per_chunk + 2 * len(dzs)

    def kernel(
        mask, counts, ratings, user, item, out_u, out_i, stats,
        rat, uf, itf, U, I, pred, scaled, acc, PU, send0, recv0, S,
        send_a, recv_a, send_b, recv_b, SA, SB,
        send_a2, recv_a2, send_b2, recv_b2,
        send_i, recv_i, mine, G, rat_sem, in_sem, ssem, rsem, gsend, grecv,
    ):
        z, c, l = lax.axis_index("row"), lax.axis_index("col"), lax.axis_index("layer")
        y, x = c // nx, c % nx

        def at(z_, y_, x_, l_):
            return (z_, y_ * nx + x_, l_)

        def xp(dx):
            return at(z, y, (x + dx) % nx, l)

        def yp(dy):
            return at(z, (y + dy) % ny, x, l)

        def lp(dl):
            return at(z, y, x, (l + dl) % nlay)

        def zp(dz):
            return at((z + dz) % nrow, y, x, l)

        def rank_of(y_, x_, l_):
            return (y_ * nx + x_) * nlay + l_

        load_u = pltpu.make_async_copy(user, uf, in_sem.at[0])
        load_i = pltpu.make_async_copy(item, itf, in_sem.at[1])
        load_u.start()
        load_i.start()
        loads = []
        for j in range(nch):
            part = pl.ds(j * width, width)
            load = pltpu.make_async_copy(ratings.at[part], rat.at[part], rat_sem.at[j])
            load.start()
            loads.append(load)

        barrier = pltpu.get_barrier_semaphore()
        peers = (
            [lp(d) for d in dls] + [xp(d) for d in dxs] + [yp(d) for d in dys] + [zp(d) for d in dzs]
        )
        for peer in peers:
            pl.semaphore_signal(barrier, inc=1, device_id=peer, device_id_type=MESH)

        me = rank_of(y, x, l)
        load_i.wait()
        I[z] = itf[...].astype(bf16).astype(idt)
        load_u.wait()
        U[me] = uf[...].astype(bf16).astype(udt)
        pl.semaphore_wait(barrier, len(peers))

        used = [0]
        pending = []

        def send(src, dst, peer):
            n = used[0]
            used[0] += 1
            copy = pltpu.make_async_remote_copy(
                src_ref=src, dst_ref=dst, send_sem=ssem.at[n], recv_sem=rsem.at[n],
                device_id=peer, device_id_type=MESH,
            )
            copy.start()
            pending.append(copy)
            return copy

        gathers_i = [send(I.at[z], I.at[z], zp(d)) for d in dzs]

        got_x, got_y, got_a, got_b, got_l = {}, {}, {}, {}, {}

        def block(j, y_, x_, l_, lo, size):
            return U.at[rank_of(y_, x_, l_), :, pl.ds(j * width + lo, size)]

        def own(j):
            b = block(j, y, x, l, 0, width)
            got_x[j] = [send(b, b, xp(d)) for d in dxs]
            got_y[j] = [send(b, b, yp(d)) for d in dys]
            got_l[j] = [send(b, b, lp(d)) for d in dls]

        def relay(j):
            got_a[j], got_b[j] = [], []
            for dx, copy in zip(dxs, got_x[j]):
                copy.wait_recv()
                sx = (x + nx - dx) % nx
                b = block(j, y, sx, l, 0, half)
                got_a[j] += [send(b, b, yp(d)) for d in dys]
            for dy, copy in zip(dys, got_y[j]):
                copy.wait_recv()
                sy = (y + ny - dy) % ny
                b = block(j, sy, x, l, half, half)
                got_b[j] += [send(b, b, xp(d)) for d in dxs]
            for dx in dxs:
                b = block(j, y, (x + nx - dx) % nx, l, 0, width)
                got_l[j] += [send(b, b, lp(d)) for d in dls]
            for dy in dys:
                b = block(j, (y + ny - dy) % ny, x, l, 0, width)
                got_l[j] += [send(b, b, lp(d)) for d in dls]

        def corner(j):
            n = 0
            for dx in dxs:
                for dy in dys:
                    got_a[j][n].wait_recv()
                    n += 1
                    b = block(j, (y + ny - dy) % ny, (x + nx - dx) % nx, l, 0, half)
                    got_l[j] += [send(b, b, lp(d)) for d in dls]
            n = 0
            for dy in dys:
                for dx in dxs:
                    got_b[j][n].wait_recv()
                    n += 1
                    b = block(j, (y + ny - dy) % ny, (x + nx - dx) % nx, l, half, half)
                    got_l[j] += [send(b, b, lp(d)) for d in dls]

        position = lax.broadcasted_iota(jnp.int32, (TILE, TILE), 0) * TILE + lax.broadcasted_iota(
            jnp.int32, (TILE, TILE), 1
        )
        got_0 = {}

        def compute(j, error):
            for copy in got_l[j]:
                copy.wait_recv()
            if j == 0:
                for copy in gathers_i:
                    copy.wait_recv()
            loads[j].wait()
            items = I[...].reshape(rank, cols).astype(bf16)
            users = U[:, :, j * width : (j + 1) * width].reshape(rank, width).astype(bf16)
            pred[...] = lax.dot_general(
                users, items, (((0,), (0,)), ((), ())), preferred_element_type=f32
            )

            def tiles(t, total):
                local = pl.ds(pl.multiple_of(t * TILE, TILE), TILE)
                whole = pl.ds(pl.multiple_of(j * width + t * TILE, TILE), TILE)
                row = j * (width // TILE) + t
                for k in range(cols // TILE):
                    lane = slice(k * TILE, (k + 1) * TILE)
                    limit = jnp.where(mask[k, row] == 1, counts[k, row], 0)
                    diff = pred[local, lane] - rat[whole, lane].astype(f32)
                    diff = jnp.where(position < limit, diff, 0.0)
                    scaled[local, lane] = diff.astype(bf16)
                    total = total + fold(diff * diff)
                return total

            error = lax.fori_loop(0, width // TILE, tiles, error)
            sc = scaled[...]
            PU[j] = lax.dot_general(
                items, sc, (((1,), (1,)), ((), ())), preferred_element_type=f32
            ).reshape(ncol, nlay, urows, width)
            got_0[j] = []
            for dl in dls:
                send0[j, dl - 1] = PU[j, :, (l + dl) % nlay].astype(udt)
                got_0[j].append(send(send0.at[j, dl - 1], recv0.at[j, dl - 1], lp(dl)))
            grad = jnp.dot(users, sc, preferred_element_type=f32).reshape(nrow, irows, cols)
            if j == 0:
                acc[...] = grad
            else:
                acc[...] += grad
            return error

        got_1a, got_1b, got_2a, got_2b = {}, {}, {}, {}

        def rs1(j):
            total = PU[j, :, l]
            for dl, copy in zip(dls, got_0[j]):
                copy.wait_recv()
                total = total + recv0[j, dl - 1].astype(f32)
            S[j] = total.reshape(ny, nx, urows, width)
            got_1a[j], got_1b[j] = [], []
            for dx in dxs:
                send_a[j, dx - 1] = S[j, :, (x + dx) % nx, :, :half].astype(udt)
                got_1a[j].append(send(send_a.at[j, dx - 1], recv_a.at[j, dx - 1], xp(dx)))
            for dy in dys:
                send_b[j, dy - 1] = S[j, (y + dy) % ny, :, :, half:].astype(udt)
                got_1b[j].append(send(send_b.at[j, dy - 1], recv_b.at[j, dy - 1], yp(dy)))

        def rs2(j):
            total = S[j, :, x, :, :half]
            for dx, copy in zip(dxs, got_1a[j]):
                copy.wait_recv()
                total = total + recv_a[j, dx - 1].astype(f32)
            SA[j] = total
            got_2a[j], got_2b[j] = [], []
            for dy in dys:
                send_a2[j, dy - 1] = SA[j, (y + dy) % ny].astype(udt)
                got_2a[j].append(send(send_a2.at[j, dy - 1], recv_a2.at[j, dy - 1], yp(dy)))
            total = S[j, y, :, :, half:]
            for dy, copy in zip(dys, got_1b[j]):
                copy.wait_recv()
                total = total + recv_b[j, dy - 1].astype(f32)
            SB[j] = total
            for dx in dxs:
                send_b2[j, dx - 1] = SB[j, (x + dx) % nx].astype(udt)
                got_2b[j].append(send(send_b2.at[j, dx - 1], recv_b2.at[j, dx - 1], xp(dx)))

        stores = []

        def rs3(j, grads):
            total = SA[j, y]
            for dy, copy in zip(dys, got_2a[j]):
                copy.wait_recv()
                total = total + recv_a2[j, dy - 1].astype(f32)
            out_u[:, j * width : j * width + half] = total
            grads = grads + fold(total * total)
            total = SB[j, x]
            for dx, copy in zip(dxs, got_2b[j]):
                copy.wait_recv()
                total = total + recv_b2[j, dx - 1].astype(f32)
            out_u[:, j * width + half : (j + 1) * width] = total
            grads = grads + fold(total * total)
            return grads

        error = jnp.zeros((8, TILE), f32)
        grads = jnp.zeros((8, TILE), f32)
        own(0)
        if nch > 1:
            own(1)
        relay(0)
        factor = fold(uf[...] * uf[...]) + fold(itf[...] * itf[...])
        got_z = []
        for j in range(nch + 3):
            if j + 2 < nch:
                own(j + 2)
            if j + 1 < nch:
                relay(j + 1)
            if j < nch:
                corner(j)
                error = compute(j, error)
            if j == nch - 1:
                for dz in dzs:
                    send_i[dz - 1] = acc[(z + dz) % nrow].astype(idt)
                    got_z.append(send(send_i.at[dz - 1], recv_i.at[dz - 1], zp(dz)))
            if 0 <= j - 1 < nch:
                rs1(j - 1)
            if 0 <= j - 2 < nch:
                rs2(j - 2)
            if 0 <= j - 3 < nch:
                grads = rs3(j - 3, grads)

        total = acc[z]
        for dz, copy in zip(dzs, got_z):
            copy.wait_recv()
            total = total + recv_i[dz - 1].astype(f32)
        out_i[...] = total
        grads = grads + fold(total * total)

        def count_of(t, total):
            for k in range(cols // TILE):
                total = total + jnp.where(mask[k, t] == 1, counts[k, t], 0)
            return total

        count = lax.fori_loop(0, rows // TILE, count_of, jnp.int32(0)).astype(f32)
        sub = lax.broadcasted_iota(jnp.int32, (8, TILE), 0)
        lane = lax.broadcasted_iota(jnp.int32, (8, TILE), 1)

        def spread(value):
            return jnp.broadcast_to(jnp.sum(value, axis=0, keepdims=True), (8, TILE))

        tile = jnp.where((sub == 3) & (lane == 0), count, 0.0)
        tile = jnp.where(sub == 0, spread(error), tile)
        tile = jnp.where(sub == 1, spread(factor), tile)
        tile = jnp.where(sub == 2, spread(grads), tile)
        mine[...] = tile
        flat = (z * ncol + c) * nlay + l
        G[flat] = tile

        def share(delta):
            to = (flat + delta) % ndev
            return pltpu.make_async_remote_copy(
                src_ref=mine, dst_ref=G.at[flat], send_sem=gsend, recv_sem=grecv,
                device_id=(to // nplane, (to // nlay) % ncol, to % nlay), device_id_type=MESH,
            )

        @pl.loop(1, ndev)
        def _(delta):
            share(delta).start()

        every = pl.ds(0, ndev - 1)
        pltpu.make_async_copy(G.at[every], G.at[every], grecv).wait()
        total = jnp.sum(G[...], axis=0)

        def pick(n):
            return jnp.sum(total[n : n + 1], axis=1, keepdims=True)

        error_sum, factor_sum, grad_sum = pick(0), pick(1), pick(2)
        observed = jnp.maximum(pick(3), 1.0)
        loss = error_sum / observed
        grad_norm = 2.0 / observed * jnp.sqrt(grad_sum + epsilon)
        rate = trust_ratio * jnp.sqrt(factor_sum + epsilon) / grad_norm
        step = rate * (2.0 / observed)
        result = jnp.where(sub == 0, loss, jnp.where(sub == 1, grad_norm, step))
        stats[...] = result
        for copy in pending:
            copy.wait_send()
        pltpu.make_async_copy(G.at[every], G.at[every], gsend).wait()

    vm = pltpu.VMEM
    dma = pltpu.SemaphoreType.DMA
    mx, my, ml, mz = max(nx - 1, 1), max(ny - 1, 1), max(nlay - 1, 1), max(nrow - 1, 1)
    smem = pl.BlockSpec(memory_space=pltpu.SMEM)
    hbm = pl.BlockSpec(memory_space=pl.ANY)
    return pl.pallas_call(
        kernel,
        out_shape=(
            jax.ShapeDtypeStruct((urows, rows), f32),
            jax.ShapeDtypeStruct((irows, cols), f32),
            jax.ShapeDtypeStruct((8, TILE), f32),
        ),
        in_specs=[smem, smem, hbm, hbm, hbm],
        out_specs=(pl.BlockSpec(memory_space=pltpu.VMEM),) * 3,
        scratch_shapes=[
            vm((rows, cols), bf16),
            vm((urows, rows), f32),
            vm((irows, cols), f32),
            vm((nplane, urows, rows), udt),
            vm((nrow, irows, cols), idt),
            vm((width, cols), f32),
            vm((width, cols), bf16),
            vm((nrow, irows, cols), f32),
            vm((nch, ncol, nlay, urows, width), f32),
            vm((nch, ml, ncol, urows, width), udt),
            vm((nch, ml, ncol, urows, width), udt),
            vm((nch, ny, nx, urows, width), f32),
            vm((nch, mx, ny, urows, half), udt),
            vm((nch, mx, ny, urows, half), udt),
            vm((nch, my, nx, urows, half), udt),
            vm((nch, my, nx, urows, half), udt),
            vm((nch, ny, urows, half), f32),
            vm((nch, nx, urows, half), f32),
            vm((nch, my, urows, half), udt),
            vm((nch, my, urows, half), udt),
            vm((nch, mx, urows, half), udt),
            vm((nch, mx, urows, half), udt),
            vm((mz, irows, cols), idt),
            vm((mz, irows, cols), idt),
            vm((8, TILE), f32),
            vm((ndev, 8, TILE), f32),
            dma((nch,)),
            dma((2,)),
            dma((n_sems,)),
            dma((n_sems,)),
            dma(()),
            dma(()),
        ],
        compiler_params=pltpu.CompilerParams(collective_id=0, has_side_effects=True),
        name="completion_step",
    )


def update(raw_user, raw_item, stats, user, item):
    def kernel(gu, gi, st, fu, fi, new_u, new_i, loss, norm):
        step = st[2:3, 0:1]
        new_i[...] = fi[...] - step * gi[...]
        new_u[...] = fu[...] - step * gu[...]
        loss[...] = st[0:1, 0:1]
        norm[...] = st[1:2, 0:1]

    f32 = jnp.float32
    whole = pl.BlockSpec(memory_space=pltpu.VMEM)
    return pl.pallas_call(
        kernel,
        out_shape=(
            jax.ShapeDtypeStruct(user.shape, f32),
            jax.ShapeDtypeStruct(item.shape, f32),
            jax.ShapeDtypeStruct((1, 1), f32),
            jax.ShapeDtypeStruct((1, 1), f32),
        ),
        in_specs=[whole] * 5,
        out_specs=(whole,) * 4,
        name="factor_update",
    )(raw_user, raw_item, stats, user, item)


def solution(mesh):
    nrow, ncol, nlay = mesh.shape["row"], mesh.shape["col"], mesh.shape["layer"]

    def body(ratings, tile_mask, tile_counts, user_factor, item_factor):
        rows, cols = ratings.shape
        rank = user_factor.shape[0] * ncol * nlay
        step = make_step(nrow, ncol, nlay, rank, rows, cols)
        raw_user, raw_item, stats = step(tile_mask.T, tile_counts.T, ratings, user_factor, item_factor)
        new_user, new_item, loss, norm = update(raw_user, raw_item, stats, user_factor, item_factor)
        return (new_user, new_item, loss[0, 0], norm[0, 0])

    return jax.shard_map(
        body,
        mesh=mesh,
        in_specs=(
            P("row", ("col", "layer")),
            P("row", ("col", "layer")),
            P("row", ("col", "layer")),
            P(("col", "layer"), "row"),
            P("row", ("col", "layer")),
        ),
        out_specs=(P(("col", "layer"), "row"), P("row", ("col", "layer")), P(), P()),
        check_vma=False,
    )
```

```python
import math

import jax
import jax.numpy as jnp
from jax import lax
from jax.experimental import pallas as pl
from jax.experimental.pallas import tpu as pltpu
from jax.sharding import PartitionSpec as P

TILE = 128
epsilon = 1e-12
trust_ratio = 0.2
MESH = pl.DeviceIdType.MESH
CHUNKS = 2
AHEAD = 2
LAG = 2


def fold(value):
    flat = value.reshape(-1, value.shape[-1])
    rows = jnp.sum(flat.reshape(flat.shape[0] // 8, 8, flat.shape[1]), axis=0)
    total = rows[:, :TILE]
    for start in range(TILE, rows.shape[1], TILE):
        total = total + rows[:, start : start + TILE]
    return total


def make_step(nrow, ncol, nlay, rank, rows, cols):
    side = math.isqrt(ncol)
    ny = nx = side
    if side * side != ncol:
        ny, nx = 1, ncol
    ndev = nrow * ncol * nlay
    nplane = ncol * nlay
    urows, irows = rank // nplane, rank // nrow
    udt = jnp.bfloat16 if urows % 16 == 0 else jnp.float32
    idt = jnp.bfloat16 if irows % 16 == 0 else jnp.float32
    f32, bf16 = jnp.float32, jnp.bfloat16
    nch = CHUNKS
    width = rows // nch

    dls, dzs = range(1, nlay), range(1, nrow)
    corners = [(dy, dx) for dy in range(ny) for dx in range(nx) if dy + dx > 0]
    per_chunk = 2 * len(corners) + len(dls) * (len(corners) + 2)
    n_sems = nch * per_chunk + 2 * len(dzs)

    def kernel(
        mask, counts, ratings, user, item, raw_user, raw_item, stats,
        rat, uf, itf, U, I, pred, scaled, acc, PU, send0, recv0, S,
        send1, recv1, out_u, out_i,
        send_i, recv_i, mine, G, rat_sem, in_sem, out_sem, ssem, rsem, gsend, grecv,
    ):
        z, c, l = lax.axis_index("row"), lax.axis_index("col"), lax.axis_index("layer")
        y, x = c // nx, c % nx

        def at(z_, y_, x_, l_):
            return (z_, y_ * nx + x_, l_)

        def cp(step):
            return at(z, (y + step[0]) % ny, (x + step[1]) % nx, l)

        def lp(dl):
            return at(z, y, x, (l + dl) % nlay)

        def zp(dz):
            return at((z + dz) % nrow, y, x, l)

        def rank_of(y_, x_, l_):
            return (y_ * nx + x_) * nlay + l_

        load_u = pltpu.make_async_copy(user, uf, in_sem.at[0])
        load_i = pltpu.make_async_copy(item, itf, in_sem.at[1])
        load_u.start()
        load_i.start()
        loads = []
        for j in range(nch):
            part = pl.ds(j * width, width)
            load = pltpu.make_async_copy(ratings.at[part], rat.at[part], rat_sem.at[j])
            load.start()
            loads.append(load)

        barrier = pltpu.get_barrier_semaphore()
        peers = (
            [zp(d) for d in dzs] + [cp(d) for d in corners] + [lp(d) for d in dls]
        )
        for peer in peers:
            pl.semaphore_signal(barrier, inc=1, device_id=peer, device_id_type=MESH)

        me = rank_of(y, x, l)
        load_i.wait()
        I[z] = itf[...].astype(bf16).astype(idt)
        load_u.wait()
        for j in range(nch):
            U[j, me] = uf[:, j * width : (j + 1) * width].astype(bf16).astype(udt)
        pl.semaphore_wait(barrier, len(peers))

        used = [0]
        pending = []

        def send(src, dst, peer):
            n = used[0]
            used[0] += 1
            copy = pltpu.make_async_remote_copy(
                src_ref=src, dst_ref=dst, send_sem=ssem.at[n], recv_sem=rsem.at[n],
                device_id=peer, device_id_type=MESH,
            )
            copy.start()
            pending.append(copy)
            return copy

        gathers_i = [send(I.at[z], I.at[z], zp(d)) for d in dzs]

        got_c, got_l = {}, {}

        def own(j):
            b = U.at[j, me]
            got_c[j] = [send(b, b, cp(d)) for d in corners]
            got_l[j] = [send(b, b, lp(d)) for d in dls]

        def relay(j):
            for (dy, dx), copy in zip(corners, got_c[j]):
                copy.wait_recv()
                b = U.at[j, rank_of((y + ny - dy) % ny, (x + nx - dx) % nx, l)]
                got_l[j] += [send(b, b, lp(d)) for d in dls]

        position = lax.broadcasted_iota(jnp.int32, (TILE, TILE), 0) * TILE + lax.broadcasted_iota(
            jnp.int32, (TILE, TILE), 1
        )
        got_0 = {}
        got_z = []

        def compute(j, error):
            for copy in got_l[j]:
                copy.wait_recv()
            if j == 0:
                for copy in gathers_i:
                    copy.wait_recv()
            loads[j].wait()
            items = I[...].reshape(rank, cols).astype(bf16)
            users = U[j].reshape(rank, width).astype(bf16)
            pred[...] = lax.dot_general(
                users, items, (((0,), (0,)), ((), ())), preferred_element_type=f32
            )

            def tiles(t, total):
                local = pl.ds(pl.multiple_of(t * TILE, TILE), TILE)
                whole = pl.ds(pl.multiple_of(j * width + t * TILE, TILE), TILE)
                row = j * (width // TILE) + t
                for k in range(cols // TILE):
                    lane = slice(k * TILE, (k + 1) * TILE)
                    limit = jnp.where(mask[k, row] == 1, counts[k, row], 0)
                    diff = pred[local, lane] - rat[whole, lane].astype(f32)
                    diff = jnp.where(position < limit, diff, 0.0)
                    scaled[local, lane] = diff.astype(bf16)
                    total = total + fold(diff * diff)
                return total

            error = lax.fori_loop(0, width // TILE, tiles, error)
            sc = scaled[...]
            grad = jnp.dot(users, sc, preferred_element_type=f32).reshape(nrow, irows, cols)
            if j == 0:
                acc[...] = grad
            else:
                acc[...] += grad
            if j == nch - 1:
                for dz in dzs:
                    send_i[dz - 1] = acc[(z + dz) % nrow].astype(idt)
                    got_z.append(send(send_i.at[dz - 1], recv_i.at[dz - 1], zp(dz)))
            PU[j] = lax.dot_general(
                items, sc, (((1,), (1,)), ((), ())), preferred_element_type=f32
            ).reshape(ncol, nlay, urows, width)
            got_0[j] = []
            for dl in dls:
                send0[j, dl - 1] = PU[j, :, (l + dl) % nlay].astype(udt)
                got_0[j].append(send(send0.at[j, dl - 1], recv0.at[j, dl - 1], lp(dl)))
            return error

        got_1 = {}

        def rs1(j):
            total = PU[j, :, l]
            for dl, copy in zip(dls, got_0[j]):
                copy.wait_recv()
                total = total + recv0[j, dl - 1].astype(f32)
            S[j] = total.reshape(ny, nx, urows, width)
            got_1[j] = []
            for n, step in enumerate(corners):
                send1[j, n] = S[j, (y + step[0]) % ny, (x + step[1]) % nx].astype(udt)
                got_1[j].append(send(send1.at[j, n], recv1.at[j, n], cp(step)))

        def rs2(j, grads):
            total = S[j, y, x]
            for n, copy in enumerate(got_1[j]):
                copy.wait_recv()
                total = total + recv1[j, n].astype(f32)
            out_u[:, j * width : (j + 1) * width] = total
            return grads + fold(total * total)

        error = jnp.zeros((8, TILE), f32)
        grads = jnp.zeros((8, TILE), f32)
        for j in range(nch):
            own(j)
        factor = fold(uf[...] * uf[...]) + fold(itf[...] * itf[...])
        for j in range(min(AHEAD, nch)):
            relay(j)
        for j in range(nch):
            error = compute(j, error)
            if j + AHEAD < nch:
                relay(j + AHEAD)
            if j >= LAG:
                rs1(j - LAG)
        for j in range(max(nch - LAG, 0), nch):
            rs1(j)
        for j in range(nch):
            grads = rs2(j, grads)

        total = acc[z]
        for dz, copy in zip(dzs, got_z):
            copy.wait_recv()
            total = total + recv_i[dz - 1].astype(f32)
        out_i[...] = total
        grads = grads + fold(total * total)

        store_u = pltpu.make_async_copy(out_u, raw_user, out_sem.at[0])
        store_i = pltpu.make_async_copy(out_i, raw_item, out_sem.at[1])
        store_u.start()
        store_i.start()

        def count_of(t, total):
            for k in range(cols // TILE):
                total = total + jnp.where(mask[k, t] == 1, counts[k, t], 0)
            return total

        count = lax.fori_loop(0, rows // TILE, count_of, jnp.int32(0)).astype(f32)
        sub = lax.broadcasted_iota(jnp.int32, (8, TILE), 0)
        lane = lax.broadcasted_iota(jnp.int32, (8, TILE), 1)

        def spread(value):
            return jnp.broadcast_to(jnp.sum(value, axis=0, keepdims=True), (8, TILE))

        tile = jnp.where((sub == 3) & (lane == 0), count, 0.0)
        tile = jnp.where(sub == 0, spread(error), tile)
        tile = jnp.where(sub == 1, spread(factor), tile)
        tile = jnp.where(sub == 2, spread(grads), tile)
        mine[...] = tile
        flat = (z * ncol + c) * nlay + l
        G[flat] = tile

        def share(delta):
            to = (flat + delta) % ndev
            return pltpu.make_async_remote_copy(
                src_ref=mine, dst_ref=G.at[flat], send_sem=gsend, recv_sem=grecv,
                device_id=(to // nplane, (to // nlay) % ncol, to % nlay), device_id_type=MESH,
            )

        @pl.loop(1, ndev)
        def _(delta):
            share(delta).start()

        every = pl.ds(0, ndev - 1)
        pltpu.make_async_copy(G.at[every], G.at[every], grecv).wait()
        total = jnp.sum(G[...], axis=0)

        def pick(n):
            return jnp.sum(total[n : n + 1], axis=1, keepdims=True)

        error_sum, factor_sum, grad_sum = pick(0), pick(1), pick(2)
        observed = jnp.maximum(pick(3), 1.0)
        loss = error_sum / observed
        grad_norm = 2.0 / observed * jnp.sqrt(grad_sum + epsilon)
        rate = trust_ratio * jnp.sqrt(factor_sum + epsilon) / grad_norm
        step = rate * (2.0 / observed)
        result = jnp.where(sub == 0, loss, jnp.where(sub == 1, grad_norm, step))
        stats[...] = result
        for copy in pending:
            copy.wait_send()
        pltpu.make_async_copy(G.at[every], G.at[every], gsend).wait()
        store_u.wait()
        store_i.wait()

    vm = pltpu.VMEM
    dma = pltpu.SemaphoreType.DMA
    mc, ml, mz = max(len(corners), 1), max(nlay - 1, 1), max(nrow - 1, 1)
    smem = pl.BlockSpec(memory_space=pltpu.SMEM)
    hbm = pl.BlockSpec(memory_space=pl.ANY)
    return pl.pallas_call(
        kernel,
        out_shape=(
            jax.ShapeDtypeStruct((urows, rows), f32),
            jax.ShapeDtypeStruct((irows, cols), f32),
            jax.ShapeDtypeStruct((8, TILE), f32),
        ),
        in_specs=[smem, smem, hbm, hbm, hbm],
        out_specs=(hbm, hbm, pl.BlockSpec(memory_space=pltpu.VMEM)),
        scratch_shapes=[
            vm((rows, cols), bf16),
            vm((urows, rows), f32),
            vm((irows, cols), f32),
            vm((nch, nplane, urows, width), udt),
            vm((nrow, irows, cols), idt),
            vm((width, cols), f32),
            vm((width, cols), bf16),
            vm((nrow, irows, cols), f32),
            vm((nch, ncol, nlay, urows, width), f32),
            vm((nch, ml, ncol, urows, width), udt),
            vm((nch, ml, ncol, urows, width), udt),
            vm((nch, ny, nx, urows, width), f32),
            vm((nch, mc, urows, width), udt),
            vm((nch, mc, urows, width), udt),
            vm((urows, rows), f32),
            vm((irows, cols), f32),
            vm((mz, irows, cols), idt),
            vm((mz, irows, cols), idt),
            vm((8, TILE), f32),
            vm((ndev, 8, TILE), f32),
            dma((nch,)),
            dma((2,)),
            dma((2,)),
            dma((n_sems,)),
            dma((n_sems,)),
            dma(()),
            dma(()),
        ],
        compiler_params=pltpu.CompilerParams(collective_id=0, has_side_effects=True),
        name="completion_step",
    )


def update(raw_user, raw_item, stats, user, item):
    def kernel(gu, gi, st, fu, fi, new_u, new_i, loss, norm):
        step = st[2:3, 0:1]
        new_i[...] = fi[...] - step * gi[...]
        new_u[...] = fu[...] - step * gu[...]
        loss[...] = st[0:1, 0:1]
        norm[...] = st[1:2, 0:1]

    f32 = jnp.float32
    whole = pl.BlockSpec(memory_space=pltpu.VMEM)
    return pl.pallas_call(
        kernel,
        out_shape=(
            jax.ShapeDtypeStruct(user.shape, f32),
            jax.ShapeDtypeStruct(item.shape, f32),
            jax.ShapeDtypeStruct((1, 1), f32),
            jax.ShapeDtypeStruct((1, 1), f32),
        ),
        in_specs=[whole] * 5,
        out_specs=(whole,) * 4,
        name="factor_update",
    )(raw_user, raw_item, stats, user, item)


def solution(mesh):
    nrow, ncol, nlay = mesh.shape["row"], mesh.shape["col"], mesh.shape["layer"]

    def body(ratings, tile_mask, tile_counts, user_factor, item_factor):
        rows, cols = ratings.shape
        rank = user_factor.shape[0] * ncol * nlay
        step = make_step(nrow, ncol, nlay, rank, rows, cols)
        raw_user, raw_item, stats = step(tile_mask.T, tile_counts.T, ratings, user_factor, item_factor)
        new_user, new_item, loss, norm = update(raw_user, raw_item, stats, user_factor, item_factor)
        return (new_user, new_item, loss[0, 0], norm[0, 0])

    return jax.shard_map(
        body,
        mesh=mesh,
        in_specs=(
            P("row", ("col", "layer")),
            P("row", ("col", "layer")),
            P("row", ("col", "layer")),
            P(("col", "layer"), "row"),
            P("row", ("col", "layer")),
        ),
        out_specs=(P(("col", "layer"), "row"), P("row", ("col", "layer")), P(), P()),
        check_vma=False,
    )
```
